32 devices in a mesh: row: 4 (over x, core), col: 8 (over z, y).
Axes of the slice: x: 2, y: 2, z: 4, core: 2. Of those that a mesh axis runs over, the one named last changes fastest.
Arguments:
- tokens: bfloat16 [1024, 2048], P('col'), may hold values from -6 to 6
- left_proj: bfloat16 [2048, 4096], P(None, 'row'), may hold values from -0.09375 to 0.09375
- teacher_up: bfloat16 [4096, 14848], P('row', 'col'), may hold values from -0.09375 to 0.09375
- right_proj: bfloat16 [14848, 7424], P('col', 'row'), may hold values from -0.046875 to 0.046875
- student_gate: bfloat16 [2048, 7424], P(None, 'row'), may hold values from -0.125 to 0.125
- target: bfloat16 [1024, 7424], P('col', 'row'), may hold values from -5 to 5
Outputs:
- grad_left: float32 [2048, 4096], P('col', 'row')
- grad_right: float32 [14848, 7424], P('col', 'row')
The draws below stay inside these ranges and needn't reach their ends.
All inputs are finite; a program needn't handle non-finite values.
Results may differ from the reference program's by a relative error of at most 0.017.
Values may be sent and summed in bfloat16 or wider, within the bound.
A program may use at most 128 MiB of HBM per device.

```python
import math
import jax
import jax.numpy as jnp
from jax import lax

D_TEACH = 4096
F_TEACH = 14848
D_STU = 2048
F_STU = 7424
TOKENS = 1024
N_ROW = 4


def level_of(stream_key, extent, pieces, least, top_value):
    loudness = 1.0
    for dim, blocks in pieces:
        heights = jax.random.uniform(jax.random.fold_in(jax.random.fold_in(stream_key, 6), dim), (blocks,), jnp.float32, least / len(pieces), top_value / len(pieces))
        loudness = loudness * jnp.repeat(jnp.exp(heights), extent[dim] // blocks).reshape((-1,) + (1,) * (len(extent) - 1 - dim))
    return loudness


def noise(own_key, shape, deviation, reach, shards=(), kind=jnp.bfloat16):
    factor_of = level_of(own_key, shape, shards, -0.22, 0.18) if shards else 1.0
    drawn = jax.random.normal(own_key, shape, jnp.float32) * deviation * factor_of
    return jnp.minimum(jnp.maximum(drawn, -reach), reach).astype(kind)


def setup_inputs(seed: int = 0) -> dict:
    key_list = jax.random.split(jax.random.key(seed), 7)
    return {
        "tokens": noise(key_list[0], (TOKENS, D_STU), 1.0, 6.0, ((0, 8),)),
        "left_proj": noise(key_list[1], (D_STU, D_TEACH), D_TEACH ** -0.5, 0.09375, ((1, 4),)),
        "teacher_up": noise(key_list[2], (D_TEACH, F_TEACH), D_TEACH ** -0.5, 0.09375, ((0, 4), (1, 8))),
        "right_proj": noise(key_list[3], (F_TEACH, F_STU), F_TEACH ** -0.5, 0.046875, ((0, 8), (1, 4))),
        "student_gate": noise(key_list[4], (D_STU, F_STU), D_STU ** -0.5, 0.125, ((1, 4),)),
        "target": noise(key_list[5], (TOKENS, F_STU), 1.0, 5.0, ((0, 8), (1, 4))),
    }


def block_sum(first_factor, second_factor, blocks):
    block_width = first_factor.shape[1] // blocks
    first_blocks = first_factor.reshape(first_factor.shape[0], blocks, block_width).transpose(1, 0, 2)
    second_blocks = second_factor.reshape(blocks, block_width, second_factor.shape[1])

    def advance(running, operands):
        partial_value = jnp.dot(operands[0], operands[1], preferred_element_type=jnp.float32)
        partial_value = lax.optimization_barrier(partial_value.astype(jnp.bfloat16)).astype(jnp.float32)
        return (running + partial_value, None)
    start_value = jnp.zeros((first_factor.shape[0], second_factor.shape[1]), jnp.float32)
    summed, _ = lax.scan(advance, start_value, (first_blocks, second_blocks))
    return summed

def reference(tokens, left_proj, teacher_up, right_proj, student_gate, target):
    hidden_proj = jnp.dot(left_proj, teacher_up, preferred_element_type=jnp.float32).astype(jnp.bfloat16)
    student_up = jnp.dot(hidden_proj, right_proj, preferred_element_type=jnp.float32).astype(jnp.bfloat16)
    gate_pre = jnp.dot(tokens, student_gate, preferred_element_type=jnp.float32)
    up_pre = jnp.dot(tokens, student_up, preferred_element_type=jnp.float32)
    gate_act = jax.nn.silu(gate_pre)
    factor = 1.0 / math.sqrt(TOKENS)
    grad_up = ((gate_act * up_pre - target.astype(jnp.float32)) * gate_act * factor).astype(jnp.bfloat16)
    grad_student = jnp.dot(tokens.T, grad_up, preferred_element_type=jnp.float32).astype(jnp.bfloat16)
    grad_right = jnp.dot(hidden_proj.T, grad_student, preferred_element_type=jnp.float32)
    grad_hidden = block_sum(grad_student, right_proj.T, N_ROW).astype(jnp.bfloat16)
    grad_left = jnp.dot(grad_hidden, teacher_up.T, preferred_element_type=jnp.float32)
    return (grad_left, grad_right)
```

```python
import math

import jax
import jax.numpy as jnp
from jax import lax
from jax.sharding import PartitionSpec as P


def mm(a, b):
    return jnp.dot(a, b, preferred_element_type=jnp.float32)


def mm_nt(a, b):
    return lax.dot_general(a, b, (((1,), (1,)), ((), ())), preferred_element_type=jnp.float32)


def mm_tn(a, b):
    return lax.dot_general(a, b, (((0,), (0,)), ((), ())), preferred_element_type=jnp.float32)


def up_gradient(gate_pre, up_pre, target, factor):
    gate_act = jax.nn.silu(gate_pre)
    return ((gate_act * up_pre - target.astype(jnp.float32)) * gate_act * factor).astype(
        jnp.bfloat16
    )


def row_sum(partial):
    part = lax.psum_scatter(partial, "row", scatter_dimension=0, tiled=True)
    return lax.all_gather(part, "row", axis=0, tiled=True)


def shards(tokens, left_proj, teacher_up, right_proj, student_gate, target):
    bf16 = jnp.bfloat16
    factor = 1.0 / math.sqrt(tokens.shape[0] * lax.axis_size("col"))
    picked = lax.all_gather(mm(tokens, left_proj).astype(bf16), "col", axis=0, tiled=True)
    token_cols = lax.all_to_all(tokens, "col", split_axis=1, concat_axis=0, tiled=True)
    gate_pre = mm(tokens, student_gate)
    features = row_sum(mm(picked, teacher_up).astype(bf16))
    up_pre = lax.psum_scatter(
        mm(features, right_proj).astype(bf16), "col", scatter_dimension=0, tiled=True
    ).astype(jnp.float32)
    grad_up = up_gradient(gate_pre, up_pre, target, factor)
    grad_all = lax.all_gather(grad_up, "col", axis=0, tiled=True)
    back = row_sum(mm_nt(grad_all, right_proj).astype(bf16))
    grad_right = mm_tn(features, grad_all)
    units = lax.psum_scatter(
        mm_nt(back, teacher_up).astype(bf16), "col", scatter_dimension=0, tiled=True
    )
    units = lax.all_gather(units, "col", axis=0, tiled=True)
    grad_left = mm_tn(token_cols, units)
    return (grad_left, grad_right)


def solution(mesh):
    return jax.shard_map(
        shards,
        mesh=mesh,
        in_specs=(
            P("col", None),
            P(None, "row"),
            P("row", "col"),
            P("col", "row"),
            P(None, "row"),
            P("col", "row"),
        ),
        out_specs=(P("col", "row"), P("col", "row")),
        check_vma=False,
    )
```

```python
import functools
import math

import jax
import jax.numpy as jnp
from jax import lax
from jax.experimental import pallas as pl
from jax.experimental.pallas import tpu as pltpu
from jax.sharding import PartitionSpec as P

MESH = pl.DeviceIdType.MESH
BF16 = jnp.bfloat16
F32 = jnp.float32
STRIP = 16


def mm(a, b):
    return jnp.dot(a, b, preferred_element_type=F32)


def mm_nt(a, b):
    return lax.dot_general(a, b, (((1,), (1,)), ((), ())), preferred_element_type=F32)


def mm_tn(a, b):
    return lax.dot_general(a, b, (((0,), (0,)), ((), ())), preferred_element_type=F32)


def block(index, size):
    return pl.ds(pl.multiple_of(index * size, size), size)


def send(src, dst, send_sem, recv_sem, axis, peer):
    return pltpu.make_async_remote_copy(
        src_ref=src,
        dst_ref=dst,
        send_sem=send_sem,
        recv_sem=recv_sem,
        device_id={axis: peer},
        device_id_type=MESH,
    )


def meet(axis, peers):
    barrier = pltpu.get_barrier_semaphore()
    for peer in peers:
        pl.semaphore_signal(barrier, inc=1, device_id={axis: peer}, device_id_type=MESH)
    pl.semaphore_wait(barrier, len(peers))


def add_strips(out, out_at, terms, rows):
    @pl.loop(0, rows // STRIP)
    def _(t):
        total = None
        for ref, at in terms:
            part = ref[pl.ds(pl.multiple_of(at + t * STRIP, STRIP), STRIP), :].astype(F32)
            total = part if total is None else total + part
        out[pl.ds(pl.multiple_of(out_at + t * STRIP, STRIP), STRIP), :] = total.astype(out.dtype)


def split_of(count):
    inner = 1
    while inner * inner * 4 <= count and count % (inner * 2) == 0:
        inner *= 2
    return count // inner, inner


def place(count):
    outer, inner = split_of(count)
    me = lax.axis_index("col")
    hi, lo = lax.div(me, inner), lax.rem(me, inner)
    return outer, inner, me, hi, lo


def gather_body(count, x, out, send_hi, recv_hi, send_lo, recv_lo):
    outer, inner, me, hi, lo = place(count)
    rows = x.shape[0]

    def at(h, l):
        return block(h * inner + l, rows)

    def to_hi(d):
        return send(x, out.at[at(hi, lo)], send_hi.at[d - 1], recv_hi.at[d - 1], "col",
                    lax.rem(hi + d, outer) * inner + lo)

    def to_lo(d, e):
        h = lax.rem(hi + outer - d, outer)
        src = x if d == 0 else out.at[at(h, lo)]
        return send(src, out.at[at(h, lo)], send_lo.at[d, e - 1], recv_lo.at[d, e - 1], "col",
                    hi * inner + lax.rem(lo + e, inner))

    for e in range(1, inner):
        to_lo(0, e).start()
    for d in range(1, outer):
        to_hi(d).start()
    out[at(hi, lo), :] = x[...]
    for d in range(1, outer):
        to_hi(d).wait_recv()
        for e in range(1, inner):
            to_lo(d, e).start()
    for d in range(outer):
        for e in range(1, inner):
            to_lo(d, e).wait()
    for d in range(1, outer):
        to_hi(d).wait_send()


def line_peers(count):
    outer, inner, me, hi, lo = place(count)
    return [lax.rem(hi + d, outer) * inner + lo for d in range(1, outer)] + [
        hi * inner + lax.rem(lo + e, inner) for e in range(1, inner)
    ]


def gather_sems(count):
    outer, inner = split_of(count)
    dma = pltpu.SemaphoreType.DMA
    far, near = (outer - 1,), (outer, max(inner - 1, 1))
    return [dma(far), dma(far), dma(near), dma(near)]


def gather_kernel(count, x, out, *sems):
    meet("col", line_peers(count))
    gather_body(count, x, out, *sems)


def gather_turn_kernel(count, x, tokens, out, turned, turn_send, turn_recv, *sems):
    me = lax.axis_index("col")
    meet("col", [lax.rem(me + d, count) for d in range(1, count)])
    rows, width = tokens.shape[0], turned.shape[1]

    def turn(d):
        peer = lax.rem(me + d, count)
        return send(tokens.at[:, block(peer, width)], turned.at[block(me, rows)],
                    turn_send.at[d - 1], turn_recv.at[d - 1], "col", peer)

    gather_body(count, x, out, *sems)
    for d in range(1, count):
        turn(d).start()
    turned[block(me, rows), :] = tokens[:, block(me, width)]
    for d in range(1, count):
        turn(d).wait()


def scatter_kernel(count, x, out, near, far, held, send_lo, recv_lo, send_hi, recv_hi):
    outer, inner, me, hi, lo = place(count)
    rows = out.shape[0]
    meet("col", line_peers(count))

    def to_lo(d, e):
        h = lax.rem(hi + d, outer)
        l = lax.rem(lo + e, inner)
        return send(x.at[block(h * inner + l, rows)], near.at[d * (inner - 1) + e - 1],
                    send_lo.at[d, e - 1], recv_lo.at[d, e - 1], "col", hi * inner + l)

    def to_hi(d):
        return send(held.at[d - 1], far.at[d - 1], send_hi.at[d - 1], recv_hi.at[d - 1], "col",
                    lax.rem(hi + d, outer) * inner + lo)

    order = list(range(1, outer)) + [0]
    for d in order:
        for e in range(1, inner):
            to_lo(d, e).start()

    def local(d):
        h = lax.rem(hi + d, outer)
        return [(x, (h * inner + lo) * rows)] + [
            (near.at[d * (inner - 1) + e - 1], 0) for e in range(1, inner)
        ]

    for d in order:
        for e in range(1, inner):
            to_lo(d, e).wait_recv()
        if d:
            add_strips(held.at[d - 1], 0, local(d), rows)
            to_hi(d).start()
    for d in range(1, outer):
        to_hi(d).wait_recv()
    add_strips(out, 0, local(0) + [(far.at[d - 1], 0) for d in range(1, outer)], rows)
    for d in range(outer):
        for e in range(1, inner):
            to_lo(d, e).wait_send()
    for d in range(1, outer):
        to_hi(d).wait_send()


def row_kernel(count, parts, x, out, near, held, far, s1, r1, s2, r2, s3, r3):
    me = lax.axis_index("row")
    pairs = count // 2
    pair, side = lax.div(me, 2), lax.rem(me, 2)
    mate = pair * 2 + 1 - side
    others = [lax.rem(pair + d, pairs) * 2 + side for d in range(1, pairs)]
    meet("row", [mate] + others)
    rows = x.shape[0] // (2 * parts)

    def at(s, k):
        return block(s * parts + k, rows)

    def first(k):
        return send(x.at[at(1 - side, k)], near.at[k], s1.at[k], r1.at[k], "row", mate)

    def across(d, k):
        return send(held.at[k], far.at[(d - 1) * parts + k], s2.at[d - 1, k], r2.at[d - 1, k],
                    "row", others[d - 1])

    def back(k):
        return send(out.at[at(side, k)], out.at[at(side, k)], s3.at[k], r3.at[k], "row", mate)

    for k in range(parts):
        first(k).start()
    for k in range(parts):
        first(k).wait_recv()
        add_strips(held.at[k], 0, [(x, (side * parts + k) * rows), (near.at[k], 0)], rows)
        for d in range(1, pairs):
            across(d, k).start()
    for k in range(parts):
        for d in range(1, pairs):
            across(d, k).wait_recv()
        add_strips(out, (side * parts + k) * rows,
                   [(held.at[k], 0)] + [(far.at[(d - 1) * parts + k], 0) for d in range(1, pairs)],
                   rows)
        back(k).start()
    for k in range(parts):
        back(k).wait()
        first(k).wait_send()
        for d in range(1, pairs):
            across(d, k).wait_send()


def call(kernel, operands, outs, scratch, collective_id):
    spec = pl.BlockSpec(memory_space=pltpu.VMEM)
    return pl.pallas_call(
        kernel,
        out_shape=outs,
        in_specs=[spec] * len(operands),
        out_specs=jax.tree.map(lambda _: spec, outs),
        scratch_shapes=scratch,
        compiler_params=pltpu.CompilerParams(
            collective_id=collective_id, has_side_effects=True
        ),
    )(*operands)


def col_gather(x, collective_id):
    n = lax.axis_size("col")
    out = jax.ShapeDtypeStruct((x.shape[0] * n, x.shape[1]), x.dtype)
    return call(functools.partial(gather_kernel, n), [x], out, gather_sems(n), collective_id)


def col_gather_turn(x, tokens, collective_id):
    n = lax.axis_size("col")
    dma = pltpu.SemaphoreType.DMA
    outs = (
        jax.ShapeDtypeStruct((x.shape[0] * n, x.shape[1]), x.dtype),
        jax.ShapeDtypeStruct((tokens.shape[0] * n, tokens.shape[1] // n), tokens.dtype),
    )
    scratch = [dma((n - 1,)), dma((n - 1,))] + gather_sems(n)
    return call(functools.partial(gather_turn_kernel, n), [x, tokens], outs, scratch, collective_id)


def col_scatter(x, dtype, collective_id):
    n = lax.axis_size("col")
    outer, inner = split_of(n)
    rows, width = x.shape[0] // n, x.shape[1]
    dma = pltpu.SemaphoreType.DMA
    near = max(inner - 1, 1)
    scratch = [
        pltpu.VMEM((outer * near, rows, width), BF16),
        pltpu.VMEM((outer - 1, rows, width), BF16),
        pltpu.VMEM((outer - 1, rows, width), BF16),
        dma((outer, near)),
        dma((outer, near)),
        dma((outer - 1,)),
        dma((outer - 1,)),
    ]
    out = jax.ShapeDtypeStruct((rows, width), dtype)
    return call(functools.partial(scatter_kernel, n), [x], out, scratch, collective_id)


def row_sum(x, collective_id, parts=4):
    n = lax.axis_size("row")
    pairs = n // 2
    rows, width = x.shape[0] // (2 * parts), x.shape[1]
    dma = pltpu.SemaphoreType.DMA
    scratch = [
        pltpu.VMEM((parts, rows, width), BF16),
        pltpu.VMEM((parts, rows, width), BF16),
        pltpu.VMEM(((pairs - 1) * parts, rows, width), BF16),
        dma((parts,)),
        dma((parts,)),
        dma((pairs - 1, parts)),
        dma((pairs - 1, parts)),
        dma((parts,)),
        dma((parts,)),
    ]
    out = jax.ShapeDtypeStruct(x.shape, x.dtype)
    return call(functools.partial(row_kernel, n, parts), [x], out, scratch, collective_id)


def up_gradient(gate_pre, up_pre, target, factor):
    gate_act = jax.nn.silu(gate_pre)
    return ((gate_act * up_pre - target.astype(F32)) * gate_act * factor).astype(BF16)


def shards(tokens, left_proj, teacher_up, right_proj, student_gate, target):
    factor = 1.0 / math.sqrt(tokens.shape[0] * lax.axis_size("col"))
    picked, token_cols = col_gather_turn(mm(tokens, left_proj).astype(BF16), tokens, 0)
    gate_pre = mm(tokens, student_gate)
    features = row_sum(mm(picked, teacher_up).astype(BF16), 1)
    up_pre = col_scatter(mm(features, right_proj).astype(BF16), F32, 2)
    grad_up = up_gradient(gate_pre, up_pre, target, factor)
    grad_all = col_gather(grad_up, 3)
    back = row_sum(mm_nt(grad_all, right_proj).astype(BF16), 1)
    grad_right = mm_tn(features, grad_all)
    units = col_gather(col_scatter(mm_nt(back, teacher_up).astype(BF16), BF16, 4), 5)
    grad_left = mm_tn(token_cols, units)
    return (grad_left, grad_right)


def solution(mesh):
    return jax.shard_map(
        shards,
        mesh=mesh,
        in_specs=(
            P("col", None),
            P(None, "row"),
            P("row", "col"),
            P("col", "row"),
            P(None, "row"),
            P("col", "row"),
        ),
        out_specs=(P("col", "row"), P("col", "row")),
        check_vma=False,
    )
```

```python
import functools
import math

import jax
import jax.numpy as jnp
from jax import lax
from jax.experimental import pallas as pl
from jax.experimental.pallas import tpu as pltpu
from jax.experimental.layout import Layout, with_layout_constraint
from jax.sharding import PartitionSpec as P

MESH = pl.DeviceIdType.MESH
BF16 = jnp.bfloat16
F32 = jnp.float32
STRIP = 16


def mm(a, b):
    return jnp.dot(a, b, preferred_element_type=F32)


def mm_nt(a, b):
    return lax.dot_general(a, b, (((1,), (1,)), ((), ())), preferred_element_type=F32)


def mm_tn(a, b):
    return lax.dot_general(a, b, (((0,), (0,)), ((), ())), preferred_element_type=F32)


def short(x):
    return with_layout_constraint(x.astype(BF16), Layout((0, 1)))


def block(index, size):
    return pl.ds(pl.multiple_of(index * size, size), size)


def send(src, dst, send_sem, recv_sem, axis, peer):
    return pltpu.make_async_remote_copy(
        src_ref=src,
        dst_ref=dst,
        send_sem=send_sem,
        recv_sem=recv_sem,
        device_id={axis: peer},
        device_id_type=MESH,
    )


def add_strips(out, out_at, terms, rows):
    @pl.loop(0, rows // STRIP)
    def _(t):
        total = None
        for ref, at in terms:
            part = ref[pl.ds(pl.multiple_of(at + t * STRIP, STRIP), STRIP), :].astype(F32)
            total = part if total is None else total + part
        out[pl.ds(pl.multiple_of(out_at + t * STRIP, STRIP), STRIP), :] = total.astype(out.dtype)


def split_of(count):
    inner = 1
    while inner * inner * 4 <= count and count % (inner * 2) == 0:
        inner *= 2
    return count // inner, inner


def place(count):
    outer, inner = split_of(count)
    me = lax.axis_index("col")
    hi, lo = lax.div(me, inner), lax.rem(me, inner)
    return outer, inner, me, hi, lo


def line_peers(count):
    outer, inner, me, hi, lo = place(count)
    return [lax.rem(hi + d, outer) * inner + lo for d in range(1, outer)] + [
        hi * inner + lax.rem(lo + e, inner) for e in range(1, inner)
    ]


def all_peers(count):
    me = lax.axis_index("col")
    return [lax.rem(me + d, count) for d in range(1, count)]


def row_place(count):
    pairs = count // 2
    me = lax.axis_index("row")
    pair, side = lax.div(me, 2), lax.rem(me, 2)
    mate = pair * 2 + 1 - side
    others = [lax.rem(pair + d, pairs) * 2 + side for d in range(1, pairs)]
    return pairs, side, mate, others


def row_peers(count):
    pairs, side, mate, others = row_place(count)
    return [mate] + others


def meet(groups):
    barrier = pltpu.get_barrier_semaphore()
    total = 0
    for axis, peers in groups:
        for peer in peers:
            pl.semaphore_signal(barrier, inc=1, device_id={axis: peer}, device_id_type=MESH)
        total += len(peers)
    pl.semaphore_wait(barrier, total)


def gather_steps(count, x, out, send_hi, recv_hi, send_lo, recv_lo):
    outer, inner, me, hi, lo = place(count)
    rows = x.shape[0]

    def at(h, l):
        return block(h * inner + l, rows)

    def to_hi(d):
        return send(x, out.at[at(hi, lo)], send_hi.at[d - 1], recv_hi.at[d - 1], "col",
                    lax.rem(hi + d, outer) * inner + lo)

    def to_lo(d, e):
        h = lax.rem(hi + outer - d, outer)
        src = x if d == 0 else out.at[at(h, lo)]
        return send(src, out.at[at(h, lo)], send_lo.at[d, e - 1], recv_lo.at[d, e - 1], "col",
                    hi * inner + lax.rem(lo + e, inner))

    for e in range(1, inner):
        to_lo(0, e).start()
    for d in range(1, outer):
        to_hi(d).start()
    out[at(hi, lo), :] = x[...]
    yield
    for d in range(1, outer):
        to_hi(d).wait_recv()
        for e in range(1, inner):
            to_lo(d, e).start()
        yield
    for d in range(outer):
        for e in range(1, inner):
            to_lo(d, e).wait()
    for d in range(1, outer):
        to_hi(d).wait_send()


def scatter_steps(count, x, out, near, far, held, send_lo, recv_lo, send_hi, recv_hi):
    outer, inner, me, hi, lo = place(count)
    rows = out.shape[0]

    def to_lo(d, e):
        h = lax.rem(hi + d, outer)
        l = lax.rem(lo + e, inner)
        return send(x.at[block(h * inner + l, rows)], near.at[d * (inner - 1) + e - 1],
                    send_lo.at[d, e - 1], recv_lo.at[d, e - 1], "col", hi * inner + l)

    def to_hi(d):
        return send(held.at[d - 1], far.at[d - 1], send_hi.at[d - 1], recv_hi.at[d - 1], "col",
                    lax.rem(hi + d, outer) * inner + lo)

    order = list(range(1, outer)) + [0]
    for d in order:
        for e in range(1, inner):
            to_lo(d, e).start()
    yield

    def local(d):
        h = lax.rem(hi + d, outer)
        return [(x, (h * inner + lo) * rows)] + [
            (near.at[d * (inner - 1) + e - 1], 0) for e in range(1, inner)
        ]

    for d in order:
        for e in range(1, inner):
            to_lo(d, e).wait_recv()
        if d:
            add_strips(held.at[d - 1], 0, local(d), rows)
            to_hi(d).start()
        yield
    for d in range(1, outer):
        to_hi(d).wait_recv()
    add_strips(out, 0, local(0) + [(far.at[d - 1], 0) for d in range(1, outer)], rows)
    yield
    for d in range(outer):
        for e in range(1, inner):
            to_lo(d, e).wait_send()
    for d in range(1, outer):
        to_hi(d).wait_send()


def turn_steps(count, tokens, turned, turn_send, turn_recv):
    me = lax.axis_index("col")
    width, rows = turned.shape[1], tokens.shape[0] // 2

    def turn(d, half):
        peer = lax.rem(me + d, count)
        return send(tokens.at[pl.ds(half * rows, rows), block(peer, width)],
                    turned.at[block(half * count + me, rows)],
                    turn_send.at[d - 1, half], turn_recv.at[d - 1, half], "col", peer)

    yield
    for half in range(2):
        for d in range(1, count):
            turn(d, half).start()
        turned[block(half * count + me, rows), :] = tokens[
            pl.ds(half * rows, rows), block(me, width)
        ]
    yield
    yield
    yield
    for half in range(2):
        for d in range(1, count):
            turn(d, half).wait()


def row_steps(count, parts, x, out, near, held, far, s1, r1, s2, r2, s3, r3):
    pairs, side, mate, others = row_place(count)
    rows = x.shape[0] // (2 * parts)

    def at(s, k):
        return block(s * parts + k, rows)

    def first(k):
        return send(x.at[at(1 - side, k)], near.at[k], s1.at[k], r1.at[k], "row", mate)

    def across(d, k):
        return send(held.at[k], far.at[(d - 1) * parts + k], s2.at[d - 1, k], r2.at[d - 1, k],
                    "row", others[d - 1])

    def back(k):
        return send(out.at[at(side, k)], out.at[at(side, k)], s3.at[k], r3.at[k], "row", mate)

    for k in range(parts):
        first(k).start()
    yield
    for k in range(parts):
        first(k).wait_recv()
        add_strips(held.at[k], 0, [(x, (side * parts + k) * rows), (near.at[k], 0)], rows)
        for d in range(1, pairs):
            across(d, k).start()
        yield
    for k in range(parts):
        for d in range(1, pairs):
            across(d, k).wait_recv()
        add_strips(out, (side * parts + k) * rows,
                   [(held.at[k], 0)] + [(far.at[(d - 1) * parts + k], 0) for d in range(1, pairs)],
                   rows)
        back(k).start()
        yield
    for k in range(parts):
        back(k).wait()
        first(k).wait_send()
        for d in range(1, pairs):
            across(d, k).wait_send()


def like(rows, width, dtype):
    return jax.ShapeDtypeStruct((rows, width), dtype)


def gather_sems(count):
    outer, inner = split_of(count)
    dma = pltpu.SemaphoreType.DMA
    far, near = (outer - 1,), (outer, max(inner - 1, 1))
    return [dma(far), dma(far), dma(near), dma(near)]


def scatter_scratch(count, rows, width):
    outer, inner = split_of(count)
    dma = pltpu.SemaphoreType.DMA
    near = max(inner - 1, 1)
    return [
        pltpu.VMEM((outer * near, rows, width), BF16),
        pltpu.VMEM((outer - 1, rows, width), BF16),
        pltpu.VMEM((outer - 1, rows, width), BF16),
        dma((outer, near)),
        dma((outer, near)),
        dma((outer - 1,)),
        dma((outer - 1,)),
    ]


def gather(x):
    n = lax.axis_size("col")
    out = like(x.shape[0] * n, x.shape[1], x.dtype)
    return "line", x, out, gather_sems(n), functools.partial(gather_steps, n)


def scatter(x, dtype):
    n = lax.axis_size("col")
    rows, width = x.shape[0] // n, x.shape[1]
    out = like(rows, width, dtype)
    return "line", x, out, scatter_scratch(n, rows, width), functools.partial(scatter_steps, n)


def col_sum(x):
    n = lax.axis_size("col")
    rows, width = x.shape[0] // n, x.shape[1]
    scratch = scatter_scratch(n, rows, width)

    def steps(x, out, total, *scr):
        yield from scatter_steps(n, x, total, *scr[: len(scratch)])
        yield from gather_steps(n, total, out, *scr[len(scratch) :])

    every = [pltpu.VMEM((rows, width), BF16)] + scratch + gather_sems(n)
    return "line", x, like(*x.shape, x.dtype), every, steps


def turn(tokens):
    n = lax.axis_size("col")
    dma = pltpu.SemaphoreType.DMA
    out = like(tokens.shape[0] * n, tokens.shape[1] // n, tokens.dtype)
    sems = [dma((n - 1, 2)), dma((n - 1, 2))]
    return "all", tokens, out, sems, functools.partial(turn_steps, n)


def row_sum(x, parts=4):
    n = lax.axis_size("row")
    pairs = n // 2
    rows, width = x.shape[0] // (2 * parts), x.shape[1]
    dma = pltpu.SemaphoreType.DMA
    scratch = [
        pltpu.VMEM((parts, rows, width), BF16),
        pltpu.VMEM((parts, rows, width), BF16),
        pltpu.VMEM(((pairs - 1) * parts, rows, width), BF16),
        dma((parts,)),
        dma((parts,)),
        dma((pairs - 1, parts)),
        dma((pairs - 1, parts)),
        dma((parts,)),
        dma((parts,)),
    ]
    return "row", x, like(*x.shape, x.dtype), scratch, functools.partial(row_steps, n, parts)


def together(collective_id, *ops):
    kinds = {op[0] for op in ops}
    col, row = lax.axis_size("col"), lax.axis_size("row")

    def kernel(*refs):
        groups = []
        if "all" in kinds:
            groups.append(("col", all_peers(col)))
        elif "line" in kinds:
            groups.append(("col", line_peers(col)))
        if "row" in kinds:
            groups.append(("row", row_peers(row)))
        meet(groups)
        n = len(ops)
        at = 2 * n
        running = []
        for i, op in enumerate(ops):
            scratch = refs[at : at + len(op[3])]
            at += len(op[3])
            running.append(op[4](refs[i], refs[n + i], *scratch))
        while running:
            running = [steps for steps in running if next(steps, running) is not running]

    spec = pl.BlockSpec(memory_space=pltpu.VMEM)
    return pl.pallas_call(
        kernel,
        out_shape=[op[2] for op in ops],
        in_specs=[spec] * len(ops),
        out_specs=[spec] * len(ops),
        scratch_shapes=[item for op in ops for item in op[3]],
        compiler_params=pltpu.CompilerParams(
            collective_id=collective_id, has_side_effects=True
        ),
    )(*[op[1] for op in ops])


def up_gradient(gate_pre, up_pre, target, factor):
    gate_act = jax.nn.silu(gate_pre)
    return ((gate_act * up_pre - target.astype(F32)) * gate_act * factor).astype(BF16)


def shards(tokens, left_proj, teacher_up, right_proj, student_gate, target):
    factor = 1.0 / math.sqrt(tokens.shape[0] * lax.axis_size("col"))
    half = tokens.shape[0] // 2

    def up(x):
        return short(mm(x, right_proj))

    def down(x):
        return short(mm_nt(x, right_proj))

    picked = short(mm(tokens, left_proj))
    picked_a, token_cols = together(0, gather(picked[:half]), turn(tokens))
    gate_pre = mm(tokens, student_gate)
    features_a, picked_b = together(
        1, row_sum(short(mm(picked_a, teacher_up))), gather(picked[half:])
    )
    features_b, up_a = together(
        2, row_sum(short(mm(picked_b, teacher_up))), scatter(up(features_a), F32)
    )
    grad_a = up_gradient(gate_pre[:half], up_a, target[:half], factor)
    up_b, all_a = together(3, scatter(up(features_b), F32), gather(grad_a))
    grad_b = up_gradient(gate_pre[half:], up_b, target[half:], factor)
    back_a, all_b = together(4, row_sum(down(all_a)), gather(grad_b))
    back_b, units_a = together(
        5, row_sum(down(all_b)), col_sum(short(mm_nt(back_a, teacher_up)))
    )
    grad_right = mm_tn(
        jnp.concatenate([features_a, features_b]), jnp.concatenate([all_a, all_b])
    )
    (units_b,) = together(6, col_sum(short(mm_nt(back_b, teacher_up))))
    grad_left = mm_tn(token_cols, jnp.concatenate([units_a, units_b]))
    return (grad_left, grad_right)


def solution(mesh):
    return jax.shard_map(
        shards,
        mesh=mesh,
        in_specs=(
            P("col", None),
            P(None, "row"),
            P("row", "col"),
            P("col", "row"),
            P(None, "row"),
            P("col", "row"),
        ),
        out_specs=(P("col", "row"), P("col", "row")),
        check_vma=False,
    )
```

```python
import functools
import math

import jax
import jax.numpy as jnp
from jax import lax
from jax.experimental import pallas as pl
from jax.experimental.pallas import tpu as pltpu
from jax.experimental.layout import Layout, with_layout_constraint
from jax.sharding import PartitionSpec as P

MESH = pl.DeviceIdType.MESH
BF16 = jnp.bfloat16
F32 = jnp.float32
STRIP = 16


def mm(a, b):
    return jnp.dot(a, b, preferred_element_type=F32)


def mm_nt(a, b):
    return lax.dot_general(a, b, (((1,), (1,)), ((), ())), preferred_element_type=F32)


def mm_tn(a, b):
    return lax.dot_general(a, b, (((0,), (0,)), ((), ())), preferred_element_type=F32)


def short(x):
    return with_layout_constraint(x.astype(BF16), Layout((0, 1)))


def block(index, size):
    return pl.ds(pl.multiple_of(index * size, size), size)


def send(src, dst, send_sem, recv_sem, axis, peer):
    return pltpu.make_async_remote_copy(
        src_ref=src,
        dst_ref=dst,
        send_sem=send_sem,
        recv_sem=recv_sem,
        device_id={axis: peer},
        device_id_type=MESH,
    )


def add_strips(out, out_at, terms, rows):
    @pl.loop(0, rows // STRIP)
    def _(t):
        total = None
        for ref, at in terms:
            part = ref[pl.ds(pl.multiple_of(at + t * STRIP, STRIP), STRIP), :].astype(F32)
            total = part if total is None else total + part
        out[pl.ds(pl.multiple_of(out_at + t * STRIP, STRIP), STRIP), :] = total.astype(out.dtype)


def split_of(count):
    inner = 1
    while inner * inner * 4 <= count and count % (inner * 2) == 0:
        inner *= 2
    return count // inner, inner


def place(count):
    outer, inner = split_of(count)
    me = lax.axis_index("col")
    hi, lo = lax.div(me, inner), lax.rem(me, inner)
    return outer, inner, me, hi, lo


def line_peers(count):
    outer, inner, me, hi, lo = place(count)
    return [lax.rem(hi + d, outer) * inner + lo for d in range(1, outer)] + [
        hi * inner + lax.rem(lo + e, inner) for e in range(1, inner)
    ]


def all_peers(count):
    me = lax.axis_index("col")
    return [lax.rem(me + d, count) for d in range(1, count)]


def row_place(count):
    pairs = count // 2
    me = lax.axis_index("row")
    pair, side = lax.div(me, 2), lax.rem(me, 2)
    mate = pair * 2 + 1 - side
    others = [lax.rem(pair + d, pairs) * 2 + side for d in range(1, pairs)]
    return pairs, side, mate, others


def row_peers(count):
    pairs, side, mate, others = row_place(count)
    return [mate] + others


def meet(groups):
    barrier = pltpu.get_barrier_semaphore()
    total = 0
    for axis, peers in groups:
        for peer in peers:
            pl.semaphore_signal(barrier, inc=1, device_id={axis: peer}, device_id_type=MESH)
        total += len(peers)
    pl.semaphore_wait(barrier, total)


def gather_steps(count, x, out, send_hi, recv_hi, send_lo, recv_lo):
    outer, inner, me, hi, lo = place(count)
    rows = x.shape[0]

    def at(h, l):
        return block(h * inner + l, rows)

    def to_hi(d):
        return send(x, out.at[at(hi, lo)], send_hi.at[d - 1], recv_hi.at[d - 1], "col",
                    lax.rem(hi + d, outer) * inner + lo)

    def to_lo(d, e):
        h = lax.rem(hi + outer - d, outer)
        src = x if d == 0 else out.at[at(h, lo)]
        return send(src, out.at[at(h, lo)], send_lo.at[d, e - 1], recv_lo.at[d, e - 1], "col",
                    hi * inner + lax.rem(lo + e, inner))

    for e in range(1, inner):
        to_lo(0, e).start()
    for d in range(1, outer):
        to_hi(d).start()
    out[at(hi, lo), :] = x[...]
    yield
    for d in range(1, outer):
        to_hi(d).wait_recv()
        for e in range(1, inner):
            to_lo(d, e).start()
        yield
    for d in range(outer):
        for e in range(1, inner):
            to_lo(d, e).wait()
    for d in range(1, outer):
        to_hi(d).wait_send()


def scatter_steps(count, x, out, near, far, held, send_lo, recv_lo, send_hi, recv_hi):
    outer, inner, me, hi, lo = place(count)
    rows = out.shape[0]

    def to_lo(d, e):
        h = lax.rem(hi + d, outer)
        l = lax.rem(lo + e, inner)
        return send(x.at[block(h * inner + l, rows)], near.at[d * (inner - 1) + e - 1],
                    send_lo.at[d, e - 1], recv_lo.at[d, e - 1], "col", hi * inner + l)

    def to_hi(d):
        return send(held.at[d - 1], far.at[d - 1], send_hi.at[d - 1], recv_hi.at[d - 1], "col",
                    lax.rem(hi + d, outer) * inner + lo)

    order = list(range(1, outer)) + [0]
    for d in order:
        for e in range(1, inner):
            to_lo(d, e).start()
    yield

    def local(d):
        h = lax.rem(hi + d, outer)
        return [(x, (h * inner + lo) * rows)] + [
            (near.at[d * (inner - 1) + e - 1], 0) for e in range(1, inner)
        ]

    for d in order:
        for e in range(1, inner):
            to_lo(d, e).wait_recv()
        if d:
            add_strips(held.at[d - 1], 0, local(d), rows)
            to_hi(d).start()
        yield
    for d in range(1, outer):
        to_hi(d).wait_recv()
    add_strips(out, 0, local(0) + [(far.at[d - 1], 0) for d in range(1, outer)], rows)
    yield
    for d in range(outer):
        for e in range(1, inner):
            to_lo(d, e).wait_send()
    for d in range(1, outer):
        to_hi(d).wait_send()


def turn_steps(count, tokens, turned, turn_send, turn_recv):
    me = lax.axis_index("col")
    width, rows = turned.shape[1], tokens.shape[0] // 2

    def turn(d, half):
        peer = lax.rem(me + d, count)
        return send(tokens.at[pl.ds(half * rows, rows), block(peer, width)],
                    turned.at[block(half * count + me, rows)],
                    turn_send.at[d - 1, half], turn_recv.at[d - 1, half], "col", peer)

    yield
    for half in range(2):
        for d in range(1, count):
            turn(d, half).start()
        turned[block(half * count + me, rows), :] = tokens[
            pl.ds(half * rows, rows), block(me, width)
        ]
    yield
    for half in range(2):
        for d in range(1, count):
            turn(d, half).wait()


def row_steps(count, parts, x, out, near, held, far, s1, r1, s2, r2, s3, r3):
    pairs, side, mate, others = row_place(count)
    rows = x.shape[0] // (2 * parts)

    def at(s, k):
        return block(s * parts + k, rows)

    def first(k):
        return send(x.at[at(1 - side, k)], near.at[k], s1.at[k], r1.at[k], "row", mate)

    def across(d, k):
        return send(held.at[k], far.at[(d - 1) * parts + k], s2.at[d - 1, k], r2.at[d - 1, k],
                    "row", others[d - 1])

    def back(k):
        return send(out.at[at(side, k)], out.at[at(side, k)], s3.at[k], r3.at[k], "row", mate)

    for k in range(parts):
        first(k).start()
    yield
    for k in range(parts):
        first(k).wait_recv()
        add_strips(held.at[k], 0, [(x, (side * parts + k) * rows), (near.at[k], 0)], rows)
        for d in range(1, pairs):
            across(d, k).start()
        yield
    for k in range(parts):
        for d in range(1, pairs):
            across(d, k).wait_recv()
        add_strips(out, (side * parts + k) * rows,
                   [(held.at[k], 0)] + [(far.at[(d - 1) * parts + k], 0) for d in range(1, pairs)],
                   rows)
        back(k).start()
        yield
    for k in range(parts):
        back(k).wait()
        first(k).wait_send()
        for d in range(1, pairs):
            across(d, k).wait_send()


def like(rows, width, dtype):
    return jax.ShapeDtypeStruct((rows, width), dtype)


def gather_sems(count):
    outer, inner = split_of(count)
    dma = pltpu.SemaphoreType.DMA
    far, near = (outer - 1,), (outer, max(inner - 1, 1))
    return [dma(far), dma(far), dma(near), dma(near)]


def scatter_scratch(count, rows, width):
    outer, inner = split_of(count)
    dma = pltpu.SemaphoreType.DMA
    near = max(inner - 1, 1)
    return [
        pltpu.VMEM((outer * near, rows, width), BF16),
        pltpu.VMEM((outer - 1, rows, width), BF16),
        pltpu.VMEM((outer - 1, rows, width), BF16),
        dma((outer, near)),
        dma((outer, near)),
        dma((outer - 1,)),
        dma((outer - 1,)),
    ]


def gather(x):
    n = lax.axis_size("col")
    out = like(x.shape[0] * n, x.shape[1], x.dtype)
    return "line", x, out, gather_sems(n), functools.partial(gather_steps, n), split_of(n)[0] + 1


def scatter(x, dtype):
    n = lax.axis_size("col")
    rows, width = x.shape[0] // n, x.shape[1]
    out = like(rows, width, dtype)
    steps = functools.partial(scatter_steps, n)
    return "line", x, out, scatter_scratch(n, rows, width), steps, split_of(n)[0] + 3


def col_sum(x):
    n = lax.axis_size("col")
    rows, width = x.shape[0] // n, x.shape[1]
    scratch = scatter_scratch(n, rows, width)

    def steps(x, out, total, *scr):
        yield from scatter_steps(n, x, total, *scr[: len(scratch)])
        yield from gather_steps(n, total, out, *scr[len(scratch) :])

    every = [pltpu.VMEM((rows, width), BF16)] + scratch + gather_sems(n)
    return "line", x, like(*x.shape, x.dtype), every, steps, 2 * split_of(n)[0] + 3


def turn(tokens):
    n = lax.axis_size("col")
    dma = pltpu.SemaphoreType.DMA
    out = like(tokens.shape[0] * n, tokens.shape[1] // n, tokens.dtype)
    sems = [dma((n - 1, 2)), dma((n - 1, 2))]
    return "all", tokens, out, sems, functools.partial(turn_steps, n), 3


def row_sum(x, parts=8):
    n = lax.axis_size("row")
    pairs = n // 2
    rows, width = x.shape[0] // (2 * parts), x.shape[1]
    dma = pltpu.SemaphoreType.DMA
    scratch = [
        pltpu.VMEM((parts, rows, width), BF16),
        pltpu.VMEM((parts, rows, width), BF16),
        pltpu.VMEM(((pairs - 1) * parts, rows, width), BF16),
        dma((parts,)),
        dma((parts,)),
        dma((pairs - 1, parts)),
        dma((pairs - 1, parts)),
        dma((parts,)),
        dma((parts,)),
    ]
    steps = functools.partial(row_steps, n, parts)
    return "row", x, like(*x.shape, x.dtype), scratch, steps, 2 * parts + 2


def together(collective_id, *ops):
    kinds = {op[0] for op in ops}
    col, row = lax.axis_size("col"), lax.axis_size("row")

    def kernel(*refs):
        groups = []
        if "all" in kinds:
            groups.append(("col", all_peers(col)))
        elif "line" in kinds:
            groups.append(("col", line_peers(col)))
        if "row" in kinds:
            groups.append(("row", row_peers(row)))
        meet(groups)
        n = len(ops)
        at = 2 * n
        running = []
        for i, op in enumerate(ops):
            scratch = refs[at : at + len(op[3])]
            at += len(op[3])
            running.append(op[4](refs[i], refs[n + i], *scratch))
        for steps in running:
            next(steps)
        taken = [1] * n
        while any(running):
            i = min(
                (i for i in range(n) if running[i]), key=lambda i: (taken[i] + 1) / ops[i][5]
            )
            taken[i] += 1
            if next(running[i], "end") == "end":
                running[i] = None

    spec = pl.BlockSpec(memory_space=pltpu.VMEM)
    return pl.pallas_call(
        kernel,
        out_shape=[op[2] for op in ops],
        in_specs=[spec] * len(ops),
        out_specs=[spec] * len(ops),
        scratch_shapes=[item for op in ops for item in op[3]],
        compiler_params=pltpu.CompilerParams(
            collective_id=collective_id, has_side_effects=True
        ),
    )(*[op[1] for op in ops])


def up_gradient(gate_pre, up_pre, target, factor):
    gate_act = jax.nn.silu(gate_pre)
    return ((gate_act * up_pre - target.astype(F32)) * gate_act * factor).astype(BF16)


def shards(tokens, left_proj, teacher_up, right_proj, student_gate, target):
    factor = 1.0 / math.sqrt(tokens.shape[0] * lax.axis_size("col"))
    half = tokens.shape[0] // 2

    def up(x):
        return short(mm(x, right_proj))

    def down(x):
        return short(mm_nt(x, right_proj))

    picked = short(mm(tokens, left_proj))
    (picked_a,) = together(0, gather(picked[:half]))
    gate_pre = mm(tokens, student_gate)
    features_a, picked_b, token_cols = together(
        1, row_sum(short(mm(picked_a, teacher_up))), gather(picked[half:]), turn(tokens)
    )
    features_b, up_a = together(
        2, row_sum(short(mm(picked_b, teacher_up))), scatter(up(features_a), F32)
    )
    grad_a = up_gradient(gate_pre[:half], up_a, target[:half], factor)
    up_b, all_a = together(3, scatter(up(features_b), F32), gather(grad_a))
    grad_b = up_gradient(gate_pre[half:], up_b, target[half:], factor)
    back_a, all_b = together(4, row_sum(down(all_a)), gather(grad_b))
    back_b, units_a = together(
        5, row_sum(down(all_b)), col_sum(short(mm_nt(back_a, teacher_up)))
    )
    grad_right = mm_tn(
        jnp.concatenate([features_a, features_b]), jnp.concatenate([all_a, all_b])
    )
    (units_b,) = together(6, col_sum(short(mm_nt(back_b, teacher_up))))
    grad_left = mm_tn(token_cols, jnp.concatenate([units_a, units_b]))
    return (grad_left, grad_right)


def solution(mesh):
    return jax.shard_map(
        shards,
        mesh=mesh,
        in_specs=(
            P("col", None),
            P(None, "row"),
            P("row", "col"),
            P("col", "row"),
            P(None, "row"),
            P("col", "row"),
        ),
        out_specs=(P("col", "row"), P("col", "row")),
        check_vma=False,
    )
```
